1024 devices in a mesh: dp: 64 (over y, x, core), tensor: 16 (over z).
Axes of the slice: x: 4, y: 8, z: 16, core: 2. Of those that a mesh axis runs over, the one named last changes fastest.
Arguments:
- token_ids: int32 [32768], P('dp'), may hold values from 0 to 511
- table: bfloat16 [512, 2560], replicated, may hold values from -729 to 729
- weights: bfloat16 [2560, 10240], P(None, 'tensor'), may hold values from -6 to 6
- targets: bfloat16 [32768, 10240], P('dp', 'tensor'), may hold values from -5.5 to 5.5
- momentum: float32 [2560, 10240], P('dp', 'tensor'), may hold values from -6 to 6
Outputs:
- new_weights: bfloat16 [2560, 10240], P(None, 'tensor')
- new_momentum: float32 [2560, 10240], P('dp', 'tensor')
The draws below stay inside these ranges and needn't reach their ends.
All inputs are finite; a program needn't handle non-finite values.
Results may differ from the reference program's by a relative error of at most 0.0052.
Values may be sent and summed in bfloat16 or wider, within the bound.
No kernel may reach another device: no remote copies, remote signals or barrier semaphores. Data moves between devices by JAX's collectives and lax.ppermute only.
A program may use at most 64 MiB of HBM per device.

```python
import math
import jax
import jax.numpy as jnp
import numpy as np
from jax import lax

D = 2560
FF = 10240
TOK_DEV = 512
TABLE_ROWS = 512
TOKENS = 32768
LEVELS = 6
N_DP = 64


def draw_table(key, part):
    base_key, factor_key = jax.random.split(key)
    base_draw = jax.random.truncated_normal(base_key, -3.0, 3.0, (TABLE_ROWS, D), jnp.float32)
    block_scale = jnp.ones((TABLE_ROWS, N_DP), jnp.float32)
    for tree_level in range(LEVELS):
        group_total = 2 ** (tree_level + 1)
        exponent = jax.random.uniform(jax.random.fold_in(factor_key, tree_level + 17), (TABLE_ROWS, group_total), jnp.float32, -1.0, 1.0)
        level_factor = jnp.exp(exponent * 1.0986123) / 1.4223
        block_scale = block_scale * jnp.repeat(level_factor, N_DP // group_total, axis=1)
    block_scale = jnp.repeat(block_scale, D // N_DP, axis=1)
    return (base_draw * block_scale / math.sqrt(D)).astype(jnp.bfloat16)


def draw_targets(key, part):
    noise_key = jax.random.fold_in(key, 101)
    noise = jax.random.truncated_normal(noise_key, -4.0, 4.0, (TOKENS, FF), jnp.float32)
    replica = jnp.arange(TOKENS, dtype=jnp.int32) // TOK_DEV
    column_block = jnp.arange(FF, dtype=jnp.int32) * 4 // FF
    flips = replica[:, None] & column_block[None, :] & 3
    parity = flips & 1 ^ flips >> 1
    offset = 1.5 * (1.0 - 2.0 * parity.astype(jnp.float32))
    return (noise + offset).astype(jnp.bfloat16)


def place_ends(array, rng, smallest, largest):
    longest = array.shape.index(max(array.shape))
    spots = []
    for shift in (0, 1):
        where = [jax.random.randint(jax.random.fold_in(rng, axis), (), 0, length) for axis, length in enumerate(array.shape)]
        where[longest] = (where[longest] + shift) % array.shape[longest]
        spots.append(tuple(where))
    return array.at[spots[0]].set(smallest).at[spots[1]].set(largest)


def shard_levels(key, dims, cuts, least, top_value):
    loudness = 1.0
    for dim, shards_of in cuts:
        steps = jax.random.uniform(jax.random.fold_in(jax.random.fold_in(key, 6), dim), (shards_of,), jnp.float32, least / len(cuts), top_value / len(cuts))
        loudness = loudness * jnp.repeat(jnp.exp(steps), dims[dim] // shards_of).reshape((-1,) + (1,) * (len(dims) - 1 - dim))
    return loudness


def rank_bounds(number_of, skew):
    weights = [(1 << 20) // math.isqrt(grade ** skew) + 1 for grade in range(1, number_of + 1)]
    spread = 1 + sum(weights) // (1 << 30)
    return np.cumsum(np.array([max(1, weight // spread) for weight in weights]))


def ranked_ids(key, extent, amount, slope):
    grid = rank_bounds(amount, slope)
    lot = jax.random.randint(jax.random.fold_in(key, 1), extent, 0, int(grid[amount - 1]))
    rank = jnp.searchsorted(jnp.asarray(grid, jnp.int32), lot, side="right")
    return jax.random.permutation(jax.random.fold_in(key, 2), amount)[rank].astype(jnp.int32)


def bell_draw(own_key, shape, deviation, bound, cuts=(), kind=jnp.bfloat16):
    values = deviation * jax.random.normal(own_key, shape, jnp.float32)
    if cuts:
        values = values * shard_levels(own_key, shape, cuts, -0.22, 0.18)
    return jnp.clip(values, -bound, bound).astype(kind)


def setup_inputs(seed: int = 0) -> dict:
    keys = jax.random.split(jax.random.key(seed), 6)
    token_ids = place_ends(ranked_ids(keys[0], (TOKENS,), TABLE_ROWS, 2), jax.random.fold_in(keys[0], 3), 0, TABLE_ROWS - 1).astype(jnp.int32)
    table = draw_table(jax.random.fold_in(keys[5], 71), 0)
    weights = bell_draw(keys[2], (D, FF), 1.0, 6.0, ((1, 16),))
    targets = draw_targets(jax.random.fold_in(keys[5], 71), 0)
    momentum = bell_draw(keys[4], (D, FF), 1.0, 6.0, ((0, 64), (1, 16)), jnp.float32)
    return {"token_ids": token_ids, "table": table, "weights": weights, "targets": targets, "momentum": momentum}


epsilon = 1e-06
momentum_decay = 0.9
learning_rate = 0.25

def gelu_tanh(values):
    return jax.nn.gelu(values, approximate=True)

def replica_grad(replica_ids, replica_targets, table, weights):
    rows_in = jnp.take(table, replica_ids, axis=0)
    preact = jnp.dot(rows_in, weights, preferred_element_type=jnp.float32)
    activated, pullback = jax.vjp(gelu_tanh, preact)
    grad_pre = pullback(activated - replica_targets.astype(jnp.float32))[0].astype(jnp.bfloat16)
    return lax.dot_general(rows_in, grad_pre, (((0,), (0,)), ((), ())), preferred_element_type=jnp.float32).astype(jnp.bfloat16)

def adasum_pair(first_vec, second_vec):
    first_vec = first_vec.astype(jnp.float32)
    second_vec = second_vec.astype(jnp.float32)
    cross_dot = jnp.sum(first_vec * second_vec)
    first_sq = jnp.sum(first_vec * first_vec)
    second_sq = jnp.sum(second_vec * second_vec)
    return (1.0 - cross_dot / (2.0 * (first_sq + epsilon))) * first_vec + (1.0 - cross_dot / (2.0 * (second_sq + epsilon))) * second_vec

def reference(token_ids, table, weights, targets, momentum):

    def subtree(members, tree_level):
        if len(members) == 1:
            replica = members[0]
            return replica_grad(token_ids[replica * TOK_DEV:(replica + 1) * TOK_DEV], targets[replica * TOK_DEV:(replica + 1) * TOK_DEV], table, weights)
        low_side = [member for member in members if member >> tree_level & 1 == 0]
        high_side = [member for member in members if member >> tree_level & 1 == 1]
        merged = adasum_pair(subtree(low_side, tree_level + 1), subtree(high_side, tree_level + 1))
        if tree_level > 0:
            merged = merged.astype(jnp.bfloat16)
        return merged
    adasum = subtree(list(range(N_DP)), 0)
    new_momentum = momentum_decay * momentum + adasum
    new_weights = (weights.astype(jnp.float32) - learning_rate * new_momentum).astype(jnp.bfloat16)
    return (new_weights, new_momentum)
```

```python
import jax
import jax.numpy as jnp
from jax import lax
from jax.experimental import pallas as pl
from jax.experimental.pallas import tpu as pltpu
from jax.sharding import PartitionSpec as P

epsilon = 1e-06
momentum_decay = 0.9
learning_rate = 0.25
LANES = 128


def gelu_tanh(values):
    return jax.nn.gelu(values, approximate=True)


def gram_kernel(slices_ref, table_ref, gram_ref):
    columns, replicas, rows = slices_ref.shape
    grads = jnp.dot(
        slices_ref[...].reshape(columns * replicas, rows),
        table_ref[...],
        preferred_element_type=jnp.float32,
    ).astype(jnp.bfloat16)
    total = jnp.zeros((replicas, replicas), jnp.float32)
    for column in range(columns):
        one = grads[column * replicas : (column + 1) * replicas]
        total += lax.dot_general(
            one, one, (((1,), (1,)), ((), ())), preferred_element_type=jnp.float32
        )
    total = jnp.concatenate([total] * (LANES // replicas), axis=1)

    @pl.when(pl.program_id(0) == 0)
    def _():
        gram_ref[...] = total

    @pl.when(pl.program_id(0) > 0)
    def _():
        gram_ref[...] += total


def gram(slices, table):
    columns, replicas, rows = slices.shape
    features = table.shape[1]
    block = 512
    return pl.pallas_call(
        gram_kernel,
        grid=(features // block,),
        in_specs=[
            pl.BlockSpec((columns, replicas, rows), lambda step: (0, 0, 0)),
            pl.BlockSpec((rows, block), lambda step: (0, step)),
        ],
        out_specs=pl.BlockSpec((replicas, LANES), lambda step: (0, 0)),
        out_shape=jax.ShapeDtypeStruct((replicas, LANES), jnp.float32),
        name="gram",
    )(slices, table)


def combine_kernel(gram_ref, slices_ref, sum_ref):
    columns, replicas, _ = slices_ref.shape
    inner = jnp.concatenate([gram_ref[...]] * (LANES // replicas), axis=0)
    row = lax.broadcasted_iota(jnp.int32, (LANES, LANES), 0)
    column = lax.broadcasted_iota(jnp.int32, (LANES, LANES), 1)
    weight = jnp.ones((LANES, 1), jnp.float32)
    for bit in reversed(range(replicas.bit_length() - 1)):
        stride = 2**bit
        own = jnp.where(row == column, inner, 0.0)
        cross = jnp.where((row + stride) % LANES == column, inner, 0.0)
        factors = []
        for axis in (1, 0):
            square = jnp.sum(own, axis=axis, keepdims=True)
            dot = jnp.sum(cross, axis=axis, keepdims=True)
            factors.append(1.0 - dot / (2.0 * (square + epsilon)))
        weight = weight * factors[0]
        scaled = factors[0] * inner * factors[1]
        scaled = scaled + pltpu.roll(scaled, stride, 0)
        inner = scaled + pltpu.roll(scaled, stride, 1)
    weight = weight[:replicas]
    for index in range(columns):
        sum_ref[pl.ds(index, 1), :] = jnp.sum(
            slices_ref[index].astype(jnp.float32) * weight, axis=0, keepdims=True
        )


def combine(gram_matrix, slices):
    columns, _, rows = slices.shape
    return pl.pallas_call(
        combine_kernel,
        out_shape=jax.ShapeDtypeStruct((columns, rows), jnp.float32),
        name="combine",
    )(gram_matrix, slices)


def exchange(value, axis):
    return lax.all_to_all(value, axis, 0, 0, tiled=True)


def share(value, axis):
    members = lax.axis_size(axis)
    return exchange(jnp.broadcast_to(value, (members, *value.shape)), axis)


def sum_everywhere(value):
    shards = lax.axis_size("tensor")
    height, width = value.shape
    part = exchange(value.reshape(shards, height // shards, width), "tensor")
    part = jnp.sum(part, axis=0)
    part = jnp.sum(share(part, "dp"), axis=0)
    return share(part, "tensor").reshape(height, width)


def update_kernel(
    features_ref, own_ref, total_ref, weights_ref, old_ref, momentum_ref, weights_out, momentum_out
):
    def product(features):
        return lax.dot_general(
            features, total_ref[...], (((1,), (1,)), ((), ())), preferred_element_type=jnp.float32
        )

    @pl.when(pl.program_id(0) == 0)
    def _():
        momentum_out[...] = momentum_decay * momentum_ref[...] + product(own_ref[...])

    step = momentum_decay * old_ref[...].astype(jnp.float32) + product(features_ref[...])
    weights_out[...] = (weights_ref[...].astype(jnp.float32) - learning_rate * step).astype(
        jnp.bfloat16
    )


def update(features, own_features, total, weights, old_momentum, momentum):
    height, hidden = weights.shape
    block = 512

    def blocked(array):
        return pl.BlockSpec((block, array.shape[1]), lambda step: (step, 0))

    def whole(array):
        return pl.BlockSpec(array.shape, lambda step: (0, 0))

    return pl.pallas_call(
        update_kernel,
        grid=(height // block,),
        in_specs=[
            blocked(features),
            whole(own_features),
            whole(total),
            blocked(weights),
            blocked(old_momentum),
            whole(momentum),
        ],
        out_specs=(blocked(weights), whole(momentum)),
        out_shape=(
            jax.ShapeDtypeStruct(weights.shape, jnp.bfloat16),
            jax.ShapeDtypeStruct(momentum.shape, jnp.float32),
        ),
        name="update",
    )(features, own_features, total, weights, old_momentum, momentum)


def body(token_ids, table, weights, targets, momentum):
    replicas = lax.axis_size("dp")
    replica_index = lax.axis_index("dp")
    owned_rows, hidden = momentum.shape
    rows = table.shape[0]
    columns = hidden // replicas
    old_momentum = lax.all_gather(momentum.astype(jnp.bfloat16), "dp", axis=0, tiled=True)

    chosen = token_ids[:, None] == lax.broadcasted_iota(jnp.int32, (token_ids.shape[0], rows), 1)
    counts = jnp.sum(chosen.astype(jnp.float32), axis=0, keepdims=True)
    wanted = lax.dot_general(
        targets,
        chosen.astype(jnp.bfloat16),
        (((0,), (0,)), ((), ())),
        preferred_element_type=jnp.float32,
    )
    preact = lax.dot_general(
        weights, table, (((0,), (1,)), ((), ())), preferred_element_type=jnp.float32
    )
    activated, pullback = jax.vjp(gelu_tanh, preact)
    row_grads = pullback(counts * activated - wanted)[0].astype(jnp.bfloat16)

    slices = exchange(row_grads.reshape(replicas, columns * rows // LANES, LANES), "dp")
    slices = slices.reshape(replicas, columns, rows).transpose(1, 0, 2)
    gram_matrix = sum_everywhere(gram(slices, table))
    total = combine(gram_matrix, slices).astype(jnp.bfloat16)
    total = share(total.reshape(columns * rows // LANES, LANES), "dp").reshape(hidden, rows)

    features = table.T
    own_features = lax.dynamic_slice_in_dim(features, replica_index * owned_rows, owned_rows, 0)
    return update(features, own_features, total, weights, old_momentum, momentum)


def solution(mesh):
    placed = (P("dp"), P(), P(None, "tensor"), P("dp", "tensor"), P("dp", "tensor"))
    return jax.shard_map(
        body,
        mesh=mesh,
        in_specs=placed,
        out_specs=(P(None, "tensor"), P("dp", "tensor")),
        check_vma=False,
    )
```

```python
import jax
import jax.numpy as jnp
from jax import lax
from jax.experimental import pallas as pl
from jax.experimental.pallas import tpu as pltpu
from jax.sharding import PartitionSpec as P

epsilon = 1e-06
momentum_decay = 0.9
learning_rate = 0.25
LANES = 128
WIDE = 256


def gelu_tanh(values):
    return jax.nn.gelu(values, approximate=True)


def gram_kernel(slices_ref, table_ref, gram_ref, total_ref):
    columns, replicas, rows = slices_ref.shape
    step = pl.program_id(0)
    grads = jnp.dot(
        slices_ref[...].reshape(columns * replicas, rows),
        table_ref[...],
        preferred_element_type=jnp.float32,
    ).astype(jnp.bfloat16)
    for start in range(0, columns * replicas, WIDE):
        some = grads[start : start + WIDE]
        height = some.shape[0]
        product = lax.dot_general(
            some, some, (((1,), (1,)), ((), ())), preferred_element_type=jnp.float32
        )
        if start == 0:
            total_ref[...] = jnp.where(step == 0, 0.0, total_ref[...]) + product
        else:
            total_ref[:height, :height] += product

    @pl.when(step == pl.num_programs(0) - 1)
    def _():
        total = jnp.zeros((replicas, replicas), jnp.float32)
        for start in range(0, WIDE, replicas):
            total += total_ref[start : start + replicas, start : start + replicas]
        gram_ref[...] = jnp.concatenate([total] * (LANES // replicas), axis=1)


def gram(slices, table):
    columns, replicas, rows = slices.shape
    features = table.shape[1]
    block = 512
    return pl.pallas_call(
        gram_kernel,
        grid=(features // block,),
        in_specs=[
            pl.BlockSpec((columns, replicas, rows), lambda step: (0, 0, 0)),
            pl.BlockSpec((rows, block), lambda step: (0, step)),
        ],
        out_specs=pl.BlockSpec((replicas, LANES), lambda step: (0, 0)),
        out_shape=jax.ShapeDtypeStruct((replicas, LANES), jnp.float32),
        scratch_shapes=[pltpu.VMEM((WIDE, WIDE), jnp.float32)],
        name="gram",
    )(slices, table)


def combine_kernel(gram_ref, slices_ref, sum_ref, flat_ref):
    columns, replicas, rows = slices_ref.shape
    inner = jnp.concatenate([gram_ref[...]] * (LANES // replicas), axis=0)
    row = lax.broadcasted_iota(jnp.int32, (LANES, LANES), 0)
    column = lax.broadcasted_iota(jnp.int32, (LANES, LANES), 1)
    weight = jnp.ones((LANES, 1), jnp.float32)
    for bit in reversed(range(replicas.bit_length() - 1)):
        stride = 2**bit
        own = jnp.where(row == column, inner, 0.0)
        cross = jnp.where((row + stride) % LANES == column, inner, 0.0)
        factors = []
        for axis in (1, 0):
            square = jnp.sum(own, axis=axis, keepdims=True)
            dot = jnp.sum(cross, axis=axis, keepdims=True)
            factors.append(1.0 - dot / (2.0 * (square + epsilon)))
        weight = weight * factors[0]
        scaled = factors[0] * inner * factors[1]
        scaled = scaled + pltpu.roll(scaled, stride, 0)
        inner = scaled + pltpu.roll(scaled, stride, 1)
    weight = weight[:replicas]
    for index in range(columns):
        total = jnp.sum(slices_ref[index].astype(jnp.float32) * weight, axis=0, keepdims=True)
        for part in range(rows // LANES):
            flat_ref[pl.ds(index * rows // LANES + part, 1), :] = total[
                :, part * LANES : (part + 1) * LANES
            ]
    flat = flat_ref[...].astype(jnp.bfloat16)
    for replica in range(replicas):
        sum_ref[replica] = flat


def combine(gram_matrix, slices):
    columns, replicas, rows = slices.shape
    height = columns * rows // LANES
    return pl.pallas_call(
        combine_kernel,
        out_shape=jax.ShapeDtypeStruct((replicas, height, LANES), jnp.bfloat16),
        scratch_shapes=[pltpu.VMEM((height, LANES), jnp.float32)],
        name="combine",
    )(gram_matrix, slices)


def exchange(value, axis):
    return lax.all_to_all(value, axis, 0, 0, tiled=True)


def share(value, axis):
    members = lax.axis_size(axis)
    return exchange(jnp.broadcast_to(value, (members, *value.shape)), axis)


def sum_everywhere(value):
    shards = lax.axis_size("tensor")
    height, width = value.shape
    part = exchange(value.reshape(shards, height // shards, width), "tensor")
    part = jnp.sum(part, axis=0)
    part = jnp.sum(share(part, "dp"), axis=0)
    return share(part, "tensor").reshape(height, width)


def update_kernel(
    first_row_ref,
    total_ref,
    features_ref,
    weights_ref,
    old_ref,
    momentum_ref,
    weights_out,
    momentum_out,
    flat_ref,
    rows_ref,
    adasum_ref,
):
    block, owned_rows = weights_out.shape[0], momentum_ref.shape[0]
    step = pl.program_id(0)
    first_row = first_row_ref[0]

    @pl.when(step == 0)
    def _():
        flat_ref[...] = total_ref[...].astype(jnp.float32).reshape(flat_ref.shape)
        height, width = rows_ref.shape
        parts = width // LANES
        for part in range(parts):
            rows_ref[:, part * LANES : (part + 1) * LANES] = flat_ref[
                pl.ds(part, height, stride=parts), :
            ].astype(jnp.bfloat16)

    adasum = lax.dot_general(
        features_ref[...],
        rows_ref[...],
        (((1,), (1,)), ((), ())),
        preferred_element_type=jnp.float32,
    )
    new_momentum = momentum_decay * old_ref[...].astype(jnp.float32) + adasum
    weights_out[...] = (
        weights_ref[...].astype(jnp.float32) - learning_rate * new_momentum
    ).astype(jnp.bfloat16)

    @pl.when(step == first_row // block)
    def _():
        adasum_ref[...] = adasum
        own = pl.ds(pl.multiple_of(first_row % block, 8), owned_rows)
        momentum_out[...] = momentum_decay * momentum_ref[...] + adasum_ref[own, :]


def update(first_row, total, features, weights, old_momentum, momentum):
    height, hidden = weights.shape
    rows = features.shape[1]
    block = 320
    blocked = pl.BlockSpec((block, hidden), lambda step, _: (step, 0))
    return pl.pallas_call(
        update_kernel,
        grid_spec=pltpu.PrefetchScalarGridSpec(
            num_scalar_prefetch=1,
            grid=(height // block,),
            in_specs=[
                pl.BlockSpec(total.shape, lambda step, _: (0, 0, 0)),
                pl.BlockSpec((block, rows), lambda step, _: (step, 0)),
                blocked,
                blocked,
                pl.BlockSpec(momentum.shape, lambda step, _: (0, 0)),
            ],
            out_specs=(blocked, pl.BlockSpec(momentum.shape, lambda step, _: (0, 0))),
            scratch_shapes=[
                pltpu.VMEM((hidden * rows // LANES, LANES), jnp.float32),
                pltpu.VMEM((hidden, rows), jnp.bfloat16),
                pltpu.VMEM((block, hidden), jnp.float32),
            ],
        ),
        out_shape=(
            jax.ShapeDtypeStruct(weights.shape, jnp.bfloat16),
            jax.ShapeDtypeStruct(momentum.shape, jnp.float32),
        ),
        name="update",
    )(
        first_row.reshape(1),
        total,
        features,
        weights,
        old_momentum,
        momentum,
    )


def body(token_ids, table, weights, targets, momentum):
    replicas = lax.axis_size("dp")
    replica_index = lax.axis_index("dp")
    owned_rows, hidden = momentum.shape
    rows = table.shape[0]
    columns = hidden // replicas
    old_momentum = lax.all_gather(momentum.astype(jnp.bfloat16), "dp", axis=0, tiled=True)

    chosen = token_ids[:, None] == lax.broadcasted_iota(jnp.int32, (token_ids.shape[0], rows), 1)
    counts = jnp.sum(chosen.astype(jnp.float32), axis=0, keepdims=True)
    wanted = lax.dot_general(
        targets,
        chosen.astype(jnp.bfloat16),
        (((0,), (0,)), ((), ())),
        preferred_element_type=jnp.float32,
    )
    preact = lax.dot_general(
        weights, table, (((0,), (1,)), ((), ())), preferred_element_type=jnp.float32
    )
    activated, pullback = jax.vjp(gelu_tanh, preact)
    row_grads = pullback(counts * activated - wanted)[0].astype(jnp.bfloat16)

    slices = exchange(row_grads.reshape(replicas, columns * rows // LANES, LANES), "dp")
    slices = slices.reshape(replicas, columns, rows).transpose(1, 0, 2)
    gram_matrix = sum_everywhere(gram(slices, table))
    total = exchange(combine(gram_matrix, slices), "dp")
    first_row = replica_index * owned_rows
    return update(first_row, total, table.T, weights, old_momentum, momentum)


def solution(mesh):
    placed = (P("dp"), P(), P(None, "tensor"), P("dp", "tensor"), P("dp", "tensor"))
    return jax.shard_map(
        body,
        mesh=mesh,
        in_specs=placed,
        out_specs=(P(None, "tensor"), P("dp", "tensor")),
        check_vma=False,
    )
```

```python
import jax
import jax.numpy as jnp
from jax import lax
from jax.experimental import pallas as pl
from jax.experimental.pallas import tpu as pltpu
from jax.sharding import Mesh
from jax.sharding import PartitionSpec as P

epsilon = 1e-06
momentum_decay = 0.9
learning_rate = 0.25
LANES = 128
WIDE = 256
FACTORS = (8, 4, 2)
CHIPS = ("y", "x")
REPLICAS = ("y", "x", "core")
CORES_FIRST = ("core", "y", "x")


def gelu_tanh(values):
    return jax.nn.gelu(values, approximate=True)


def gram_kernel(slices_ref, kernel_ref, gram_ref):
    columns, replicas, rows = slices_ref.shape
    values = slices_ref[...].reshape(columns * replicas, rows)
    high = kernel_ref[...].astype(jnp.bfloat16)
    low = (kernel_ref[...] - high.astype(jnp.float32)).astype(jnp.bfloat16)
    images = (
        jnp.dot(values, high, preferred_element_type=jnp.float32)
        + jnp.dot(values, low, preferred_element_type=jnp.float32)
    ).astype(jnp.bfloat16)
    total = jnp.zeros((replicas, replicas), jnp.float32)
    for start in range(0, columns * replicas, WIDE):
        products = lax.dot_general(
            values[start : start + WIDE],
            images[start : start + WIDE],
            (((1,), (1,)), ((), ())),
            preferred_element_type=jnp.float32,
        )
        for own in range(0, products.shape[0], replicas):
            total += products[own : own + replicas, own : own + replicas]
    height = replicas // 4
    for half in range(2):
        first = 2 * half * height
        gram_ref[half] = jnp.concatenate(
            [total[first : first + height], total[first + height : first + 2 * height]], axis=1
        )


def gram(slices, kernel):
    replicas = slices.shape[1]
    return pl.pallas_call(
        gram_kernel,
        out_shape=jax.ShapeDtypeStruct((2, replicas // 4, 2 * replicas), jnp.float32),
        name="gram",
    )(slices, kernel)


def combine_kernel(gram_ref, slices_ref, sum_ref, flat_ref):
    columns, replicas, rows = slices_ref.shape
    full = []
    for half in range(2):
        for side in range(2):
            lines = gram_ref[half, :, side * replicas : (side + 1) * replicas]
            full.append(jnp.concatenate([lines] * (LANES // replicas), axis=1))
    inner = jnp.concatenate(full * (LANES // replicas), axis=0)
    row = lax.broadcasted_iota(jnp.int32, (LANES, LANES), 0)
    column = lax.broadcasted_iota(jnp.int32, (LANES, LANES), 1)

    def partner(values, stride, axis):
        place = column if axis else row
        ahead = pltpu.roll(values, stride, axis)
        behind = pltpu.roll(values, LANES - stride, axis)
        return jnp.where(place & stride != 0, ahead, behind)

    weight = jnp.ones((LANES, 1), jnp.float32)
    strides = [2**bit for bit in reversed(range(replicas.bit_length() - 2))] + [replicas // 2]
    for stride in strides:
        own = jnp.where(row == column, inner, 0.0)
        cross = jnp.where(row ^ stride == column, inner, 0.0)
        factors = []
        for axis in (1, 0):
            square = jnp.sum(own, axis=axis, keepdims=True)
            dot = jnp.sum(cross, axis=axis, keepdims=True)
            factors.append(1.0 - dot / (2.0 * (square + epsilon)))
        weight = weight * factors[0]
        scaled = factors[0] * inner * factors[1]
        scaled = scaled + partner(scaled, stride, 0)
        inner = scaled + partner(scaled, stride, 1)
    weight = weight[:replicas]
    for index in range(columns):
        total = jnp.sum(slices_ref[index].astype(jnp.float32) * weight, axis=0, keepdims=True)
        for part in range(rows // LANES):
            flat_ref[pl.ds(index * rows // LANES + part, 1), :] = total[
                :, part * LANES : (part + 1) * LANES
            ]
    flat = flat_ref[...].astype(jnp.bfloat16)
    for copy in range(sum_ref.shape[0]):
        sum_ref[copy] = flat


def combine(gram_matrix, slices):
    columns, replicas, rows = slices.shape
    height = columns * rows // LANES
    return pl.pallas_call(
        combine_kernel,
        out_shape=jax.ShapeDtypeStruct((replicas // 2, height, LANES), jnp.bfloat16),
        scratch_shapes=[pltpu.VMEM((height, LANES), jnp.float32)],
        name="combine",
    )(gram_matrix, slices)


def exchange(value, axis):
    return lax.all_to_all(value, axis, 0, 0, tiled=True)


def share(value, axis):
    members = lax.axis_size(axis)
    return exchange(jnp.broadcast_to(value, (members, *value.shape)), axis)


def sum_everywhere(halves):
    part = jnp.sum(exchange(halves, "core"), axis=0)
    part = jnp.sum(share(part, "z"), axis=0)
    part = jnp.sum(share(part, CHIPS), axis=0)
    return share(part, "core")


def update_kernel(
    first_row_ref,
    total_ref,
    features_ref,
    weights_ref,
    old_ref,
    momentum_ref,
    weights_out,
    momentum_out,
    flat_ref,
    rows_ref,
    adasum_ref,
):
    block, owned_rows = weights_out.shape[0], momentum_ref.shape[0]
    step = pl.program_id(0)
    first_row = first_row_ref[0]

    @pl.when(step == 0)
    def _():
        flat_ref[...] = total_ref[...].astype(jnp.float32).reshape(flat_ref.shape)
        height, width = rows_ref.shape
        parts = width // LANES
        for part in range(parts):
            rows_ref[:, part * LANES : (part + 1) * LANES] = flat_ref[
                pl.ds(part, height, stride=parts), :
            ].astype(jnp.bfloat16)

    adasum = lax.dot_general(
        features_ref[...],
        rows_ref[...],
        (((1,), (1,)), ((), ())),
        preferred_element_type=jnp.float32,
    )
    new_momentum = momentum_decay * old_ref[...].astype(jnp.float32) + adasum
    weights_out[...] = (
        weights_ref[...].astype(jnp.float32) - learning_rate * new_momentum
    ).astype(jnp.bfloat16)

    @pl.when(step == first_row // block)
    def _():
        adasum_ref[...] = adasum
        own = pl.ds(pl.multiple_of(first_row % block, 8), owned_rows)
        momentum_out[...] = momentum_decay * momentum_ref[...] + adasum_ref[own, :]


def update(first_row, total, features, weights, old_momentum, momentum):
    height, hidden = weights.shape
    rows = features.shape[1]
    block = 640
    blocked = pl.BlockSpec((block, hidden), lambda step, _: (step, 0))
    return pl.pallas_call(
        update_kernel,
        grid_spec=pltpu.PrefetchScalarGridSpec(
            num_scalar_prefetch=1,
            grid=(height // block,),
            in_specs=[
                pl.BlockSpec(total.shape, lambda step, _: (0, 0, 0, 0)),
                pl.BlockSpec((block, rows), lambda step, _: (step, 0)),
                blocked,
                blocked,
                pl.BlockSpec(momentum.shape, lambda step, _: (0, 0)),
            ],
            out_specs=(blocked, pl.BlockSpec(momentum.shape, lambda step, _: (0, 0))),
            scratch_shapes=[
                pltpu.VMEM((hidden * rows // LANES, LANES), jnp.float32),
                pltpu.VMEM((hidden, rows), jnp.bfloat16),
                pltpu.VMEM((block, hidden), jnp.float32),
            ],
        ),
        out_shape=(
            jax.ShapeDtypeStruct(weights.shape, jnp.bfloat16),
            jax.ShapeDtypeStruct(momentum.shape, jnp.float32),
        ),
        name="update",
    )(
        first_row.reshape(1),
        total,
        features,
        weights,
        old_momentum,
        momentum,
    )


def body(token_ids, table, weights, targets, momentum):
    replicas = lax.axis_size(REPLICAS)
    owned_rows, hidden = momentum.shape
    rows = table.shape[0]
    columns = hidden // replicas

    chosen = token_ids[:, None] == lax.broadcasted_iota(jnp.int32, (token_ids.shape[0], rows), 1)
    counts = jnp.sum(chosen.astype(jnp.float32), axis=0, keepdims=True)
    wanted = lax.dot_general(
        targets,
        chosen.astype(jnp.bfloat16),
        (((0,), (0,)), ((), ())),
        preferred_element_type=jnp.float32,
    )
    preact = lax.dot_general(
        weights, table, (((0,), (1,)), ((), ())), preferred_element_type=jnp.float32
    )
    activated, pullback = jax.vjp(gelu_tanh, preact)
    row_grads = pullback(counts * activated - wanted)[0].astype(jnp.bfloat16)

    row_grads, table, momentum = lax.optimization_barrier((row_grads, table, momentum))
    old_momentum = lax.all_gather(momentum.astype(jnp.bfloat16), REPLICAS, axis=0, tiled=True)
    slices = exchange(row_grads.reshape(replicas, columns * rows // LANES, LANES), CORES_FIRST)
    slices = slices.reshape(replicas, columns, rows).transpose(1, 0, 2)
    kernel = lax.dot_general(
        table, table, (((1,), (1,)), ((), ())), preferred_element_type=jnp.float32
    )
    total = combine(sum_everywhere(gram(slices, kernel)), slices)
    total = share(exchange(total, CHIPS), "core")
    first_row = lax.axis_index(REPLICAS) * owned_rows
    return update(first_row, total, table.T, weights, old_momentum, momentum)


def solution(mesh):
    axes = Mesh(mesh.devices.reshape(*FACTORS, -1), (*REPLICAS, "z"))
    placed = (P(REPLICAS), P(), P(None, "z"), P(REPLICAS, "z"), P(REPLICAS, "z"))
    return jax.shard_map(
        body,
        mesh=axes,
        in_specs=placed,
        out_specs=(P(None, "z"), P(REPLICAS, "z")),
        check_vma=False,
    )
```

```python
import jax
import jax.numpy as jnp
from jax import lax
from jax.experimental import pallas as pl
from jax.experimental.pallas import tpu as pltpu
from jax.sharding import Mesh
from jax.sharding import PartitionSpec as P

epsilon = 1e-06
momentum_decay = 0.9
learning_rate = 0.25
LANES = 128
WIDE = 256
FACTORS = (8, 4, 2)
CHIPS = ("y", "x")
REPLICAS = ("y", "x", "core")
CORES_FIRST = ("core", "y", "x")


def gelu_tanh(values):
    return jax.nn.gelu(values, approximate=True)


def rows_kernel(ids_ref, preact_ref, targets_ref, blocks_ref, flat_ref):
    hidden, rows = preact_ref.shape
    tokens = targets_ref.shape[0]
    parts = rows // LANES
    targets = targets_ref[...].T
    ones = jnp.ones((8, tokens), jnp.bfloat16)
    over_tokens = (((1,), (1,)), ((), ()))
    for part in range(parts):
        row = part * LANES + lax.broadcasted_iota(jnp.int32, (LANES, tokens), 0)
        chosen = (row == ids_ref[...]).astype(jnp.float32).astype(jnp.bfloat16)
        counts = lax.dot_general(ones, chosen, over_tokens, preferred_element_type=jnp.float32)
        wanted = lax.dot_general(targets, chosen, over_tokens, preferred_element_type=jnp.float32)
        preact = preact_ref[:, part * LANES : (part + 1) * LANES]
        activated, pullback = jax.vjp(gelu_tanh, preact)
        flat_ref[pl.ds(part, hidden, stride=parts), :] = pullback(counts[:1] * activated - wanted)[0]
    blocks_ref[...] = flat_ref[...].reshape(blocks_ref.shape).astype(jnp.bfloat16)


def row_blocks(token_ids, preact, targets, replicas):
    hidden, rows = preact.shape
    height = hidden * rows // LANES
    return pl.pallas_call(
        rows_kernel,
        out_shape=jax.ShapeDtypeStruct((replicas, height // replicas, LANES), jnp.bfloat16),
        scratch_shapes=[pltpu.VMEM((height, LANES), jnp.float32)],
        name="rows",
    )(token_ids.reshape(1, -1), preact, targets)


def gram_kernel(blocks_ref, kernel_ref, gram_ref, flat_ref, values_ref):
    replicas, height, _ = blocks_ref.shape
    rows = kernel_ref.shape[0]
    parts = rows // LANES
    flat_ref[...] = blocks_ref[...].astype(jnp.float32).reshape(flat_ref.shape)
    for index in range(height):
        column, part = index // parts, index % parts
        values_ref[
            column * replicas : (column + 1) * replicas, part * LANES : (part + 1) * LANES
        ] = flat_ref[pl.ds(index, replicas, stride=height), :].astype(jnp.bfloat16)
    values = values_ref[...]
    high = kernel_ref[...].astype(jnp.bfloat16)
    low = (kernel_ref[...] - high.astype(jnp.float32)).astype(jnp.bfloat16)
    images = (
        jnp.dot(values, high, preferred_element_type=jnp.float32)
        + jnp.dot(values, low, preferred_element_type=jnp.float32)
    ).astype(jnp.bfloat16)
    total = jnp.zeros((replicas, replicas), jnp.float32)
    for start in range(0, values.shape[0], WIDE):
        products = lax.dot_general(
            values[start : start + WIDE],
            images[start : start + WIDE],
            (((1,), (1,)), ((), ())),
            preferred_element_type=jnp.float32,
        )
        for own in range(0, products.shape[0], replicas):
            total += products[own : own + replicas, own : own + replicas]
    lines = replicas // 4
    for half in range(2):
        first = 2 * half * lines
        gram_ref[half] = jnp.concatenate(
            [total[first : first + lines], total[first + lines : first + 2 * lines]], axis=1
        )


def gram(blocks, kernel):
    replicas, height, _ = blocks.shape
    rows = kernel.shape[0]
    return pl.pallas_call(
        gram_kernel,
        out_shape=jax.ShapeDtypeStruct((2, replicas // 4, 2 * replicas), jnp.float32),
        scratch_shapes=[
            pltpu.VMEM((replicas * height, LANES), jnp.float32),
            pltpu.VMEM((replicas * height * LANES // rows, rows), jnp.bfloat16),
        ],
        name="gram",
    )(blocks, kernel)


def combine_kernel(gram_ref, blocks_ref, sum_ref, weight_ref):
    replicas, height, _ = blocks_ref.shape
    chips = gram_ref.shape[0] // 2
    halves = [jnp.sum(gram_ref[half * chips : (half + 1) * chips], axis=0) for half in range(2)]
    full = []
    for half in range(2):
        for side in range(2):
            lines = halves[half][:, side * replicas : (side + 1) * replicas]
            full.append(jnp.concatenate([lines] * (LANES // replicas), axis=1))
    inner = jnp.concatenate(full * (LANES // replicas), axis=0)
    row = lax.broadcasted_iota(jnp.int32, (LANES, LANES), 0)
    column = lax.broadcasted_iota(jnp.int32, (LANES, LANES), 1)

    def partner(values, stride, axis):
        place = column if axis else row
        ahead = pltpu.roll(values, stride, axis)
        behind = pltpu.roll(values, LANES - stride, axis)
        return jnp.where(place & stride != 0, ahead, behind)

    weight = jnp.ones((LANES, 1), jnp.float32)
    strides = [2**bit for bit in reversed(range(replicas.bit_length() - 2))] + [replicas // 2]
    for stride in strides:
        own = jnp.where(row == column, inner, 0.0)
        cross = jnp.where(row ^ stride == column, inner, 0.0)
        factors = []
        for axis in (1, 0):
            square = jnp.sum(own, axis=axis, keepdims=True)
            dot = jnp.sum(cross, axis=axis, keepdims=True)
            factors.append(1.0 - dot / (2.0 * (square + epsilon)))
        weight = weight * factors[0]
        scaled = factors[0] * inner * factors[1]
        scaled = scaled + partner(scaled, stride, 0)
        inner = scaled + partner(scaled, stride, 1)
    weight_ref[...] = jnp.broadcast_to(weight, weight_ref.shape)
    total = jnp.zeros((height, LANES), jnp.float32)
    for replica in range(replicas):
        total += blocks_ref[replica].astype(jnp.float32) * weight_ref[pl.ds(replica, 1), :]
    total = total.astype(jnp.bfloat16)
    for copy in range(sum_ref.shape[0]):
        sum_ref[copy] = total


def combine(gram_parts, blocks):
    replicas, height, _ = blocks.shape
    return pl.pallas_call(
        combine_kernel,
        out_shape=jax.ShapeDtypeStruct((replicas // 2, height, LANES), jnp.bfloat16),
        scratch_shapes=[pltpu.VMEM((LANES, LANES), jnp.float32)],
        name="combine",
    )(gram_parts, blocks)


def exchange(value, axis):
    return lax.all_to_all(value, axis, 0, 0, tiled=True)


def share(value, axis):
    members = lax.axis_size(axis)
    return exchange(jnp.broadcast_to(value, (members, *value.shape)), axis)


def update_kernel(
    place_ref,
    own_ref,
    other_ref,
    features_ref,
    weights_ref,
    old_ref,
    momentum_ref,
    weights_out,
    momentum_out,
    flat_ref,
    rows_ref,
    adasum_ref,
):
    block, owned_rows = weights_out.shape[0], momentum_ref.shape[0]
    step = pl.program_id(0)
    first_row = place_ref[0]

    @pl.when(step == 0)
    def _():
        half = flat_ref.shape[0] // 2
        for blocks_ref, core in ((own_ref, place_ref[1]), (other_ref, 1 - place_ref[1])):
            flat_ref[pl.ds(pl.multiple_of(core * half, half), half), :] = (
                blocks_ref[...].astype(jnp.float32).reshape(half, LANES)
            )
        height, width = rows_ref.shape
        parts = width // LANES
        for part in range(parts):
            rows_ref[:, part * LANES : (part + 1) * LANES] = flat_ref[
                pl.ds(part, height, stride=parts), :
            ].astype(jnp.bfloat16)

    adasum = lax.dot_general(
        features_ref[...],
        rows_ref[...],
        (((1,), (1,)), ((), ())),
        preferred_element_type=jnp.float32,
    )
    new_momentum = momentum_decay * old_ref[...].astype(jnp.float32) + adasum
    weights_out[...] = (
        weights_ref[...].astype(jnp.float32) - learning_rate * new_momentum
    ).astype(jnp.bfloat16)

    @pl.when(step == first_row // block)
    def _():
        adasum_ref[...] = adasum
        own = pl.ds(pl.multiple_of(first_row % block, 8), owned_rows)
        momentum_out[...] = momentum_decay * momentum_ref[...] + adasum_ref[own, :]


def update(place, own, other, features, weights, old_momentum, momentum):
    height, hidden = weights.shape
    rows = features.shape[1]
    block = 640
    blocked = pl.BlockSpec((block, hidden), lambda step, _: (step, 0))
    return pl.pallas_call(
        update_kernel,
        grid_spec=pltpu.PrefetchScalarGridSpec(
            num_scalar_prefetch=1,
            grid=(height // block,),
            in_specs=[
                pl.BlockSpec(own.shape, lambda step, _: (0, 0, 0)),
                pl.BlockSpec(own.shape, lambda step, _: (0, 0, 0)),
                pl.BlockSpec((block, rows), lambda step, _: (step, 0)),
                blocked,
                blocked,
                pl.BlockSpec(momentum.shape, lambda step, _: (0, 0)),
            ],
            out_specs=(blocked, pl.BlockSpec(momentum.shape, lambda step, _: (0, 0))),
            scratch_shapes=[
                pltpu.VMEM((hidden * rows // LANES, LANES), jnp.float32),
                pltpu.VMEM((hidden, rows), jnp.bfloat16),
                pltpu.VMEM((block, hidden), jnp.float32),
            ],
        ),
        out_shape=(
            jax.ShapeDtypeStruct(weights.shape, jnp.bfloat16),
            jax.ShapeDtypeStruct(momentum.shape, jnp.float32),
        ),
        name="update",
    )(
        place,
        own,
        other,
        features,
        weights,
        old_momentum,
        momentum,
    )


def body(token_ids, table, weights, targets, momentum):
    replicas = lax.axis_size(REPLICAS)
    owned_rows, hidden = momentum.shape
    preact = lax.dot_general(
        weights, table, (((0,), (1,)), ((), ())), preferred_element_type=jnp.float32
    )
    blocks = row_blocks(token_ids, preact, targets, replicas)
    blocks, table, momentum = lax.optimization_barrier((blocks, table, momentum))
    old_momentum = lax.all_gather(momentum.astype(jnp.bfloat16), REPLICAS, axis=0, tiled=True)
    blocks = exchange(blocks, CORES_FIRST)
    kernel = lax.dot_general(
        table, table, (((1,), (1,)), ((), ())), preferred_element_type=jnp.float32
    )
    part = jnp.sum(exchange(gram(blocks, kernel), "core"), axis=0)
    part = jnp.sum(share(part, "z"), axis=0)
    own = exchange(combine(share(part, CORES_FIRST), blocks), CHIPS)
    other = lax.ppermute(own, "core", [(0, 1), (1, 0)])
    place = jnp.stack([lax.axis_index(REPLICAS) * owned_rows, lax.axis_index("core")])
    return update(place, own, other, table.T, weights, old_momentum, momentum)


def solution(mesh):
    axes = Mesh(mesh.devices.reshape(*FACTORS, -1), (*REPLICAS, "z"))
    placed = (P(REPLICAS), P(), P(None, "z"), P(REPLICAS, "z"), P(REPLICAS, "z"))
    return jax.shard_map(
        body,
        mesh=axes,
        in_specs=placed,
        out_specs=(P(None, "z"), P(REPLICAS, "z")),
        check_vma=False,
    )
```

```python
import jax
import jax.numpy as jnp
from jax import lax
from jax.experimental import pallas as pl
from jax.experimental.pallas import tpu as pltpu
from jax.sharding import Mesh
from jax.sharding import PartitionSpec as P

epsilon = 1e-06
momentum_decay = 0.9
learning_rate = 0.25
LANES = 128
WIDE = 256
FACTORS = (8, 4, 2)
CHIPS = ("y", "x")
REPLICAS = ("y", "x", "core")
CORES_FIRST = ("core", "y", "x")
SCALARS = pl.BlockSpec(memory_space=pltpu.SMEM)
VECTORS = pl.BlockSpec(memory_space=pltpu.VMEM)


def gelu_tanh(values):
    return jax.nn.gelu(values, approximate=True)


def rows_kernel(ids_ref, preact_ref, targets_ref, blocks_ref, flat_ref):
    hidden, rows = preact_ref.shape
    tokens = targets_ref.shape[0]
    parts = rows // LANES
    targets = targets_ref[...].T
    ones = jnp.ones((8, tokens), jnp.bfloat16)
    over_tokens = (((1,), (1,)), ((), ()))
    for part in range(parts):
        row = part * LANES + lax.broadcasted_iota(jnp.int32, (LANES, tokens), 0)
        chosen = (row == ids_ref[...]).astype(jnp.float32).astype(jnp.bfloat16)
        counts = lax.dot_general(ones, chosen, over_tokens, preferred_element_type=jnp.float32)
        wanted = lax.dot_general(targets, chosen, over_tokens, preferred_element_type=jnp.float32)
        preact = preact_ref[:, part * LANES : (part + 1) * LANES]
        activated, pullback = jax.vjp(gelu_tanh, preact)
        flat_ref[pl.ds(part, hidden, stride=parts), :] = pullback(counts[:1] * activated - wanted)[0]
    blocks_ref[...] = flat_ref[...].reshape(blocks_ref.shape).astype(jnp.bfloat16)


def row_blocks(token_ids, preact, targets, replicas):
    hidden, rows = preact.shape
    height = hidden * rows // LANES
    return pl.pallas_call(
        rows_kernel,
        out_shape=jax.ShapeDtypeStruct((replicas, height // replicas, LANES), jnp.bfloat16),
        scratch_shapes=[pltpu.VMEM((height, LANES), jnp.float32)],
        name="rows",
    )(token_ids.reshape(1, -1), preact, targets)


def gram_kernel(place_ref, blocks_ref, kernel_ref, kept_ref, sent_ref, flat_ref, values_ref):
    replicas, height, _ = blocks_ref.shape
    rows = kernel_ref.shape[0]
    parts = rows // LANES
    flat_ref[...] = blocks_ref[...].astype(jnp.float32).reshape(flat_ref.shape)
    for index in range(height):
        column, part = index // parts, index % parts
        values_ref[
            column * replicas : (column + 1) * replicas, part * LANES : (part + 1) * LANES
        ] = flat_ref[pl.ds(index, replicas, stride=height), :].astype(jnp.bfloat16)
    values = values_ref[...]
    high = kernel_ref[...].astype(jnp.bfloat16)
    low = (kernel_ref[...] - high.astype(jnp.float32)).astype(jnp.bfloat16)
    images = (
        jnp.dot(values, high, preferred_element_type=jnp.float32)
        + jnp.dot(values, low, preferred_element_type=jnp.float32)
    ).astype(jnp.bfloat16)
    total = jnp.zeros((replicas, replicas), jnp.float32)
    for start in range(0, values.shape[0], WIDE):
        products = lax.dot_general(
            values[start : start + WIDE],
            images[start : start + WIDE],
            (((1,), (1,)), ((), ())),
            preferred_element_type=jnp.float32,
        )
        for own in range(0, products.shape[0], replicas):
            total += products[own : own + replicas, own : own + replicas]
    lines = replicas // 4
    quarters = [total[quarter * lines : (quarter + 1) * lines] for quarter in range(4)]
    upper = jnp.concatenate(quarters[:2], axis=1)
    lower = jnp.concatenate(quarters[2:], axis=1)
    first = place_ref[1] == 0
    kept_ref[...] = jnp.where(first, upper, lower)
    sent_ref[...] = jnp.where(first, lower, upper)


def gram(place, blocks, kernel):
    replicas, height, _ = blocks.shape
    rows = kernel.shape[0]
    return pl.pallas_call(
        gram_kernel,
        in_specs=[SCALARS, VECTORS, VECTORS],
        out_shape=[jax.ShapeDtypeStruct((replicas // 4, 2 * replicas), jnp.float32)] * 2,
        scratch_shapes=[
            pltpu.VMEM((replicas * height, LANES), jnp.float32),
            pltpu.VMEM((replicas * height * LANES // rows, rows), jnp.bfloat16),
        ],
        name="gram",
    )(place, blocks, kernel)


def combine_kernel(place_ref, own_ref, other_ref, blocks_ref, sum_ref, weight_ref):
    replicas, height, _ = blocks_ref.shape
    first = place_ref[1] == 0
    own, other = own_ref[...], other_ref[...]
    halves = [jnp.where(first, own, other), jnp.where(first, other, own)]
    full = []
    for half in range(2):
        for side in range(2):
            lines = halves[half][:, side * replicas : (side + 1) * replicas]
            full.append(jnp.concatenate([lines] * (LANES // replicas), axis=1))
    inner = jnp.concatenate(full * (LANES // replicas), axis=0)
    row = lax.broadcasted_iota(jnp.int32, (LANES, LANES), 0)
    column = lax.broadcasted_iota(jnp.int32, (LANES, LANES), 1)

    def partner(values, stride, axis):
        place = column if axis else row
        ahead = pltpu.roll(values, stride, axis)
        behind = pltpu.roll(values, LANES - stride, axis)
        return jnp.where(place & stride != 0, ahead, behind)

    weight = jnp.ones((LANES, 1), jnp.float32)
    strides = [2**bit for bit in reversed(range(replicas.bit_length() - 2))] + [replicas // 2]
    for stride in strides:
        own = jnp.where(row == column, inner, 0.0)
        cross = jnp.where(row ^ stride == column, inner, 0.0)
        factors = []
        for axis in (1, 0):
            square = jnp.sum(own, axis=axis, keepdims=True)
            dot = jnp.sum(cross, axis=axis, keepdims=True)
            factors.append(1.0 - dot / (2.0 * (square + epsilon)))
        weight = weight * factors[0]
        scaled = factors[0] * inner * factors[1]
        scaled = scaled + partner(scaled, stride, 0)
        inner = scaled + partner(scaled, stride, 1)
    weight_ref[...] = jnp.broadcast_to(weight, weight_ref.shape)
    total = jnp.zeros((height, LANES), jnp.float32)
    for replica in range(replicas):
        total += blocks_ref[replica].astype(jnp.float32) * weight_ref[pl.ds(replica, 1), :]
    total = total.astype(jnp.bfloat16)
    for copy in range(sum_ref.shape[0]):
        sum_ref[copy] = total


def combine(place, own, other, blocks):
    replicas, height, _ = blocks.shape
    return pl.pallas_call(
        combine_kernel,
        in_specs=[SCALARS, VECTORS, VECTORS, VECTORS],
        out_shape=jax.ShapeDtypeStruct((replicas // 2, height, LANES), jnp.bfloat16),
        scratch_shapes=[pltpu.VMEM((LANES, LANES), jnp.float32)],
        name="combine",
    )(place, own, other, blocks)


def exchange(value, axis):
    return lax.all_to_all(value, axis, 0, 0, tiled=True)


def share(value, axis):
    members = lax.axis_size(axis)
    return exchange(jnp.broadcast_to(value, (members, *value.shape)), axis)


def swap_cores(value):
    return lax.ppermute(value, "core", [(0, 1), (1, 0)])


def transpose_kernel(table_ref, features_ref):
    features_ref[...] = table_ref[...].T


def transpose(table):
    rows, features = table.shape
    block = 640
    return pl.pallas_call(
        transpose_kernel,
        grid=(features // block,),
        in_specs=[pl.BlockSpec((rows, block), lambda step: (0, step))],
        out_specs=pl.BlockSpec((block, rows), lambda step: (step, 0)),
        out_shape=jax.ShapeDtypeStruct((features, rows), table.dtype),
        name="transpose",
    )(table)


def update_kernel(
    place_ref,
    own_ref,
    other_ref,
    features_ref,
    weights_ref,
    old_ref,
    momentum_ref,
    weights_out,
    momentum_out,
    flat_ref,
    rows_ref,
    adasum_ref,
):
    block, owned_rows = weights_out.shape[0], momentum_ref.shape[0]
    step = pl.program_id(0)
    first_row = place_ref[0]

    @pl.when(step == 0)
    def _():
        half = flat_ref.shape[0] // 2
        for blocks_ref, core in ((own_ref, place_ref[1]), (other_ref, 1 - place_ref[1])):
            flat_ref[pl.ds(pl.multiple_of(core * half, half), half), :] = (
                blocks_ref[...].astype(jnp.float32).reshape(half, LANES)
            )
        height, width = rows_ref.shape
        parts = width // LANES
        for part in range(parts):
            rows_ref[:, part * LANES : (part + 1) * LANES] = flat_ref[
                pl.ds(part, height, stride=parts), :
            ].astype(jnp.bfloat16)

    adasum = lax.dot_general(
        features_ref[...],
        rows_ref[...],
        (((1,), (1,)), ((), ())),
        preferred_element_type=jnp.float32,
    )
    new_momentum = momentum_decay * old_ref[...].astype(jnp.float32) + adasum
    weights_out[...] = (
        weights_ref[...].astype(jnp.float32) - learning_rate * new_momentum
    ).astype(jnp.bfloat16)

    @pl.when(step == first_row // block)
    def _():
        adasum_ref[...] = adasum
        own = pl.ds(pl.multiple_of(first_row % block, 8), owned_rows)
        momentum_out[...] = momentum_decay * momentum_ref[...] + adasum_ref[own, :]


def update(place, own, other, features, weights, old_momentum, momentum):
    height, hidden = weights.shape
    rows = features.shape[1]
    block = 640
    blocked = pl.BlockSpec((block, hidden), lambda step, _: (step, 0))
    return pl.pallas_call(
        update_kernel,
        grid_spec=pltpu.PrefetchScalarGridSpec(
            num_scalar_prefetch=1,
            grid=(height // block,),
            in_specs=[
                pl.BlockSpec(own.shape, lambda step, _: (0, 0, 0)),
                pl.BlockSpec(own.shape, lambda step, _: (0, 0, 0)),
                pl.BlockSpec((block, rows), lambda step, _: (step, 0)),
                blocked,
                blocked,
                pl.BlockSpec(momentum.shape, lambda step, _: (0, 0)),
            ],
            out_specs=(blocked, pl.BlockSpec(momentum.shape, lambda step, _: (0, 0))),
            scratch_shapes=[
                pltpu.VMEM((hidden * rows // LANES, LANES), jnp.float32),
                pltpu.VMEM((hidden, rows), jnp.bfloat16),
                pltpu.VMEM((block, hidden), jnp.float32),
            ],
        ),
        out_shape=(
            jax.ShapeDtypeStruct(weights.shape, jnp.bfloat16),
            jax.ShapeDtypeStruct(momentum.shape, jnp.float32),
        ),
        name="update",
    )(
        place,
        own,
        other,
        features,
        weights,
        old_momentum,
        momentum,
    )


def body(token_ids, table, weights, targets, momentum):
    replicas = lax.axis_size(REPLICAS)
    owned_rows, hidden = momentum.shape
    preact = lax.dot_general(
        weights, table, (((0,), (1,)), ((), ())), preferred_element_type=jnp.float32
    )
    blocks = row_blocks(token_ids, preact, targets, replicas)
    blocks, table, momentum = lax.optimization_barrier((blocks, table, momentum))
    old_momentum = lax.all_gather(momentum.astype(jnp.bfloat16), REPLICAS, axis=0, tiled=True)
    blocks = exchange(blocks, CORES_FIRST)
    kernel = lax.dot_general(
        table, table, (((1,), (1,)), ((), ())), preferred_element_type=jnp.float32
    )
    place = jnp.stack([lax.axis_index(REPLICAS) * owned_rows, lax.axis_index("core")])
    kept, sent = gram(place, blocks, kernel)
    part = jnp.sum(share(kept + swap_cores(sent), "z"), axis=0)
    part = jnp.sum(share(part, CHIPS), axis=0)
    total = combine(place, part, swap_cores(part), blocks)
    total, table = lax.optimization_barrier((total, table))
    own, features = lax.optimization_barrier((exchange(total, CHIPS), transpose(table)))
    return update(place, own, swap_cores(own), features, weights, old_momentum, momentum)


def solution(mesh):
    axes = Mesh(mesh.devices.reshape(*FACTORS, -1), (*REPLICAS, "z"))
    placed = (P(REPLICAS), P(), P(None, "z"), P(REPLICAS, "z"), P(REPLICAS, "z"))
    return jax.shard_map(
        body,
        mesh=axes,
        in_specs=placed,
        out_specs=(P(None, "z"), P(REPLICAS, "z")),
        check_vma=False,
    )
```

```python
import jax
import jax.numpy as jnp
from jax import lax
from jax.experimental import pallas as pl
from jax.experimental.pallas import tpu as pltpu
from jax.sharding import Mesh
from jax.sharding import PartitionSpec as P

epsilon = 1e-06
momentum_decay = 0.9
learning_rate = 0.25
LANES = 128
WIDE = 256
FACTORS = (8, 4, 2)
CHIPS = ("y", "x")
REPLICAS = ("y", "x", "core")
CORES_FIRST = ("core", "y", "x")
SMALL = pltpu.CompilerParams(vmem_limit_bytes=24 * 2**20)
SCALARS = pl.BlockSpec(memory_space=pltpu.SMEM)
VECTORS = pl.BlockSpec(memory_space=pltpu.VMEM)


def gelu_tanh(values):
    return jax.nn.gelu(values, approximate=True)


def rows_kernel(ids_ref, preact_ref, targets_ref, blocks_ref, flat_ref):
    hidden, rows = preact_ref.shape
    tokens = targets_ref.shape[0]
    parts = rows // LANES
    targets = targets_ref[...].T
    ones = jnp.ones((8, tokens), jnp.bfloat16)
    over_tokens = (((1,), (1,)), ((), ()))
    for part in range(parts):
        row = part * LANES + lax.broadcasted_iota(jnp.int32, (LANES, tokens), 0)
        chosen = (row == ids_ref[...]).astype(jnp.float32).astype(jnp.bfloat16)
        counts = lax.dot_general(ones, chosen, over_tokens, preferred_element_type=jnp.float32)
        wanted = lax.dot_general(targets, chosen, over_tokens, preferred_element_type=jnp.float32)
        preact = preact_ref[:, part * LANES : (part + 1) * LANES]
        activated, pullback = jax.vjp(gelu_tanh, preact)
        flat_ref[pl.ds(part, hidden, stride=parts), :] = pullback(counts[:1] * activated - wanted)[0]
    blocks_ref[...] = flat_ref[...].reshape(blocks_ref.shape).astype(jnp.bfloat16)


def row_blocks(token_ids, preact, targets, replicas):
    hidden, rows = preact.shape
    height = hidden * rows // LANES
    return pl.pallas_call(
        rows_kernel,
        out_shape=jax.ShapeDtypeStruct((replicas, height // replicas, LANES), jnp.bfloat16),
        scratch_shapes=[pltpu.VMEM((height, LANES), jnp.float32)],
        compiler_params=SMALL,
        name="rows",
    )(token_ids.reshape(1, -1), preact, targets)


def gram_kernel(place_ref, blocks_ref, kernel_ref, kept_ref, sent_ref, flat_ref, values_ref):
    replicas, height, _ = blocks_ref.shape
    rows = kernel_ref.shape[0]
    parts = rows // LANES
    flat_ref[...] = blocks_ref[...].astype(jnp.float32).reshape(flat_ref.shape)
    for index in range(height):
        column, part = index // parts, index % parts
        values_ref[
            column * replicas : (column + 1) * replicas, part * LANES : (part + 1) * LANES
        ] = flat_ref[pl.ds(index, replicas, stride=height), :].astype(jnp.bfloat16)
    values = values_ref[...]
    high = kernel_ref[...].astype(jnp.bfloat16)
    low = (kernel_ref[...] - high.astype(jnp.float32)).astype(jnp.bfloat16)
    images = (
        jnp.dot(values, high, preferred_element_type=jnp.float32)
        + jnp.dot(values, low, preferred_element_type=jnp.float32)
    ).astype(jnp.bfloat16)
    total = jnp.zeros((replicas, replicas), jnp.float32)
    for start in range(0, values.shape[0], WIDE):
        products = lax.dot_general(
            values[start : start + WIDE],
            images[start : start + WIDE],
            (((1,), (1,)), ((), ())),
            preferred_element_type=jnp.float32,
        )
        for own in range(0, products.shape[0], replicas):
            total += products[own : own + replicas, own : own + replicas]
    lines = replicas // 4
    quarters = [total[quarter * lines : (quarter + 1) * lines] for quarter in range(4)]
    upper = jnp.concatenate(quarters[:2], axis=1)
    lower = jnp.concatenate(quarters[2:], axis=1)
    first = place_ref[1] == 0
    kept_ref[...] = jnp.where(first, upper, lower)
    sent_ref[...] = jnp.where(first, lower, upper)


def gram(place, blocks, kernel):
    replicas, height, _ = blocks.shape
    rows = kernel.shape[0]
    return pl.pallas_call(
        gram_kernel,
        in_specs=[SCALARS, VECTORS, VECTORS],
        out_shape=[jax.ShapeDtypeStruct((replicas // 4, 2 * replicas), jnp.float32)] * 2,
        scratch_shapes=[
            pltpu.VMEM((replicas * height, LANES), jnp.float32),
            pltpu.VMEM((replicas * height * LANES // rows, rows), jnp.bfloat16),
        ],
        compiler_params=SMALL,
        name="gram",
    )(place, blocks, kernel)


def combine_kernel(place_ref, own_ref, other_ref, blocks_ref, sum_ref, weight_ref):
    replicas, height, _ = blocks_ref.shape
    first = place_ref[1] == 0
    own, other = own_ref[...], other_ref[...]
    halves = [jnp.where(first, own, other), jnp.where(first, other, own)]
    full = []
    for half in range(2):
        for side in range(2):
            lines = halves[half][:, side * replicas : (side + 1) * replicas]
            full.append(jnp.concatenate([lines] * (LANES // replicas), axis=1))
    inner = jnp.concatenate(full * (LANES // replicas), axis=0)
    row = lax.broadcasted_iota(jnp.int32, (LANES, LANES), 0)
    column = lax.broadcasted_iota(jnp.int32, (LANES, LANES), 1)

    def partner(values, stride, axis):
        place = column if axis else row
        ahead = pltpu.roll(values, stride, axis)
        behind = pltpu.roll(values, LANES - stride, axis)
        return jnp.where(place & stride != 0, ahead, behind)

    weight = jnp.ones((LANES, 1), jnp.float32)
    strides = [2**bit for bit in reversed(range(replicas.bit_length() - 2))] + [replicas // 2]
    for stride in strides:
        own = jnp.where(row == column, inner, 0.0)
        cross = jnp.where(row ^ stride == column, inner, 0.0)
        factors = []
        for axis in (1, 0):
            square = jnp.sum(own, axis=axis, keepdims=True)
            dot = jnp.sum(cross, axis=axis, keepdims=True)
            factors.append(1.0 - dot / (2.0 * (square + epsilon)))
        weight = weight * factors[0]
        scaled = factors[0] * inner * factors[1]
        scaled = scaled + partner(scaled, stride, 0)
        inner = scaled + partner(scaled, stride, 1)
    weight_ref[...] = jnp.broadcast_to(weight, weight_ref.shape)
    total = jnp.zeros((height, LANES), jnp.float32)
    for replica in range(replicas):
        total += blocks_ref[replica].astype(jnp.float32) * weight_ref[pl.ds(replica, 1), :]
    total = total.astype(jnp.bfloat16)
    for copy in range(sum_ref.shape[0]):
        sum_ref[copy] = total


def combine(place, own, other, blocks):
    replicas, height, _ = blocks.shape
    return pl.pallas_call(
        combine_kernel,
        in_specs=[SCALARS, VECTORS, VECTORS, VECTORS],
        out_shape=jax.ShapeDtypeStruct((replicas // 2, height, LANES), jnp.bfloat16),
        scratch_shapes=[pltpu.VMEM((LANES, LANES), jnp.float32)],
        compiler_params=SMALL,
        name="combine",
    )(place, own, other, blocks)


def exchange(value, axis):
    return lax.all_to_all(value, axis, 0, 0, tiled=True)


def share(value, axis):
    members = lax.axis_size(axis)
    return exchange(jnp.broadcast_to(value, (members, *value.shape)), axis)


def swap_cores(value):
    return lax.ppermute(value, "core", [(0, 1), (1, 0)])


def transpose_kernel(table_ref, features_ref):
    features_ref[...] = table_ref[...].T


def transpose(table):
    rows, features = table.shape
    block = 640
    return pl.pallas_call(
        transpose_kernel,
        grid=(features // block,),
        in_specs=[pl.BlockSpec((rows, block), lambda step: (0, step))],
        out_specs=pl.BlockSpec((block, rows), lambda step: (step, 0)),
        out_shape=jax.ShapeDtypeStruct((features, rows), table.dtype),
        name="transpose",
    )(table)


def update_kernel(
    place_ref,
    own_ref,
    other_ref,
    features_ref,
    weights_ref,
    old_ref,
    momentum_ref,
    weights_out,
    momentum_out,
    flat_ref,
    rows_ref,
    adasum_ref,
):
    block, owned_rows = weights_out.shape[0], momentum_ref.shape[0]
    step = pl.program_id(0)
    first_row = place_ref[0]

    @pl.when(step == 0)
    def _():
        half = flat_ref.shape[0] // 2
        for blocks_ref, core in ((own_ref, place_ref[1]), (other_ref, 1 - place_ref[1])):
            flat_ref[pl.ds(pl.multiple_of(core * half, half), half), :] = (
                blocks_ref[...].astype(jnp.float32).reshape(half, LANES)
            )
        height, width = rows_ref.shape
        parts = width // LANES
        for part in range(parts):
            rows_ref[:, part * LANES : (part + 1) * LANES] = flat_ref[
                pl.ds(part, height, stride=parts), :
            ].astype(jnp.bfloat16)

    adasum = lax.dot_general(
        features_ref[...],
        rows_ref[...],
        (((1,), (1,)), ((), ())),
        preferred_element_type=jnp.float32,
    )
    new_momentum = momentum_decay * old_ref[...].astype(jnp.float32) + adasum
    weights_out[...] = (
        weights_ref[...].astype(jnp.float32) - learning_rate * new_momentum
    ).astype(jnp.bfloat16)

    @pl.when(step == first_row // block)
    def _():
        adasum_ref[...] = adasum
        own = pl.ds(pl.multiple_of(first_row % block, 8), owned_rows)
        momentum_out[...] = momentum_decay * momentum_ref[...] + adasum_ref[own, :]


def update(place, own, other, features, weights, old_momentum, momentum):
    height, hidden = weights.shape
    rows = features.shape[1]
    block = 640
    blocked = pl.BlockSpec((block, hidden), lambda step, _: (step, 0))
    return pl.pallas_call(
        update_kernel,
        grid_spec=pltpu.PrefetchScalarGridSpec(
            num_scalar_prefetch=1,
            grid=(height // block,),
            in_specs=[
                pl.BlockSpec(own.shape, lambda step, _: (0, 0, 0)),
                pl.BlockSpec(own.shape, lambda step, _: (0, 0, 0)),
                pl.BlockSpec((block, rows), lambda step, _: (step, 0)),
                blocked,
                blocked,
                pl.BlockSpec(momentum.shape, lambda step, _: (0, 0)),
            ],
            out_specs=(blocked, pl.BlockSpec(momentum.shape, lambda step, _: (0, 0))),
            scratch_shapes=[
                pltpu.VMEM((hidden * rows // LANES, LANES), jnp.float32),
                pltpu.VMEM((hidden, rows), jnp.bfloat16),
                pltpu.VMEM((block, hidden), jnp.float32),
            ],
        ),
        out_shape=(
            jax.ShapeDtypeStruct(weights.shape, jnp.bfloat16),
            jax.ShapeDtypeStruct(momentum.shape, jnp.float32),
        ),
        name="update",
    )(
        place,
        own,
        other,
        features,
        weights,
        old_momentum,
        momentum,
    )


def body(token_ids, table, weights, targets, momentum):
    replicas = lax.axis_size(REPLICAS)
    owned_rows, hidden = momentum.shape
    preact = lax.dot_general(
        weights, table, (((0,), (1,)), ((), ())), preferred_element_type=jnp.float32
    )
    blocks = row_blocks(token_ids, preact, targets, replicas)
    blocks, table, momentum = lax.optimization_barrier((blocks, table, momentum))
    old_momentum = lax.all_gather(momentum.astype(jnp.bfloat16), REPLICAS, axis=0, tiled=True)
    blocks = exchange(blocks, CORES_FIRST)
    kernel = lax.dot_general(
        table, table, (((1,), (1,)), ((), ())), preferred_element_type=jnp.float32
    )
    place = jnp.stack([lax.axis_index(REPLICAS) * owned_rows, lax.axis_index("core")])
    kept, sent = gram(place, blocks, kernel)
    part = jnp.sum(share(kept + swap_cores(sent), "z"), axis=0)
    part = jnp.sum(share(part, CHIPS), axis=0)
    total = combine(place, part, swap_cores(part), blocks)
    total, table = lax.optimization_barrier((total, table))
    own, features = lax.optimization_barrier((exchange(total, CHIPS), transpose(table)))
    return update(place, own, swap_cores(own), features, weights, old_momentum, momentum)


def solution(mesh):
    axes = Mesh(mesh.devices.reshape(*FACTORS, -1), (*REPLICAS, "z"))
    placed = (P(REPLICAS), P(), P(None, "z"), P(REPLICAS, "z"), P(REPLICAS, "z"))
    return jax.shard_map(
        body,
        mesh=axes,
        in_specs=placed,
        out_specs=(P(None, "z"), P(REPLICAS, "z")),
        check_vma=False,
    )
```
